32 devices in a mesh: groups: 2 (over x), ctx: 8 (over z, y), tp: 2 (over core).
Axes of the slice: x: 2, y: 2, z: 4, core: 2. Of those that a mesh axis runs over, the one named last changes fastest.
Arguments:
- enc_input: bfloat16 [2048, 4096], P(('groups', 'ctx')), parts along dimension 0, may hold values from -6 to 6
- enc_query: bfloat16 [2048, 1024], P(('groups', 'ctx'), 'tp'), parts along dimension 0
- enc_key: bfloat16 [2048, 1024], P(('groups', 'ctx'), 'tp'), parts along dimension 0
- enc_value: bfloat16 [2048, 1024], P(('groups', 'ctx'), 'tp'), parts along dimension 0, may hold values from -6 to 6
- seq_length: int32 [2], P('groups'), parts along dimension 0, may hold values from 256 to 1024
- attn_out_weight: bfloat16 [1024, 4096], P('tp'), may hold values from -0.1875 to 0.1875
- enc_gain: bfloat16 [4096], replicated, may hold values from 0.25 to 1.75
- cross_key_weight: bfloat16 [4096, 1024], P('ctx', 'tp'), may hold values from -0.09375 to 0.09375
- cross_value_weight: bfloat16 [4096, 1024], P('ctx', 'tp'), may hold values from -0.09375 to 0.09375
- embed_table: bfloat16 [32128, 4096], P('tp', 'ctx')
- dec_ids: int32 [32, 2], P('groups'), parts along dimension 0, may hold values from 0 to 32127
- dec_gain: bfloat16 [4096], P('ctx'), may hold values from 0.25 to 1.75
- cross_query_weight: bfloat16 [4096, 1024], P('ctx', 'tp')
- cross_out_weight: bfloat16 [1024, 4096], P('tp', 'ctx'), may hold values from -0.1875 to 0.1875
Outputs:
- cross_keys: bfloat16 [16, 128, 1024], P(('groups', 'ctx'), None, 'tp'), parts along dimension 0
- cross_values: bfloat16 [16, 128, 1024], P(('groups', 'ctx'), None, 'tp'), parts along dimension 0
- decoded: bfloat16 [32, 2, 4096], P('groups', None, 'ctx'), parts along dimension 0
The draws below stay inside these ranges and needn't reach their ends.
There are 2 independent parts, one for each index of `groups`. The reference program is written for one: setup_inputs(seed, part) draws one part's arguments, and reference() takes and returns one part's arrays. A program takes and returns all parts, laid end to end along the dimension named above; an argument that names none is the same for every part. Nothing has to cross between parts.
Inputs may be any that keep to these rules, and one draw needn't show every extreme that they name: `seq_length`: the input's real length.
All inputs are finite; a program needn't handle non-finite values.
Results may differ from the reference program's by a relative error of at most 0.04.
Values may be sent and summed in bfloat16 or wider, within the bound.
A program may use at most 128 MiB of HBM per device.

```python
import math
import jax
import jax.numpy as jnp
import numpy as np
from jax import lax

D = 4096
HEADS = 8
HD = 128
VOCAB = 32128
BEAMS = 16
INNER = 1024
SEQ = 1024
N_CTX = 8


def attention_pair(key):
    queries = 1.7 * jnp.clip(jax.random.normal(jax.random.fold_in(key, 11), (SEQ, INNER), jnp.float32), -6.0, 6.0)
    keys = 1.7 * jnp.clip(jax.random.normal(jax.random.fold_in(key, 12), (SEQ, INNER), jnp.float32), -6.0, 6.0)
    return (queries, keys)


def draw_enc_query(key, part):
    return attention_pair(key)[0].astype(jnp.bfloat16)


def draw_enc_key(key, part):
    return attention_pair(key)[1].astype(jnp.bfloat16)


def draw_embed_table(key, part):
    row_scale = jnp.exp(jax.random.uniform(jax.random.fold_in(key, 21), (VOCAB, 1), jnp.float32, math.log(0.4), math.log(1.6)))
    col_scale = jnp.exp(jnp.linspace(math.log(0.4), math.log(1.6), D, dtype=jnp.float32))[None, :]
    base = 0.8 * jnp.clip(jax.random.normal(jax.random.fold_in(key, 22), (VOCAB, D), jnp.float32), -3.0, 3.0)
    return (base * row_scale * col_scale).astype(jnp.bfloat16)


def draw_cross_query_weight(key, part):
    spread = 6.0 / math.sqrt(D)
    base = jnp.clip(jax.random.normal(jax.random.fold_in(key, 33), (D, INNER), jnp.float32), -5.0, 5.0)
    return (base * spread).astype(jnp.bfloat16)


def touch_ends(values, rng, least, largest):
    longest = values.shape.index(max(values.shape))
    spots = []
    for shift in (0, 1):
        where = [jax.random.randint(jax.random.fold_in(rng, axis), (), 0, length) for axis, length in enumerate(values.shape)]
        where[longest] = (where[longest] + shift) % values.shape[longest]
        spots.append(tuple(where))
    return values.at[spots[0]].set(least).at[spots[1]].set(largest)


def shard_levels(stream_key, extent, pieces, least, top_value):
    gain, own = 1.0, jax.random.fold_in(stream_key, 6)
    for axis_at, blocks in pieces:
        heights = jnp.exp(jax.random.uniform(jax.random.fold_in(own, axis_at), (blocks,), jnp.float32, least / len(pieces), top_value / len(pieces)))
        gain = gain * jnp.repeat(heights, extent[axis_at] // blocks).reshape([-1 if axis == axis_at else 1 for axis in range(len(extent))])
    return gain


def rank_table(amount, lean):
    weights = [(1 << 20) // math.isqrt(standing ** lean) + 1 for standing in range(1, amount + 1)]
    deviation = 1 + sum(weights) // (1 << 30)
    return np.cumsum(np.array([max(1, weight // deviation) for weight in weights]))


def ranked_ids(rng, shape, amount, lean):
    table = rank_table(amount, lean)
    pick = jax.random.randint(jax.random.fold_in(rng, 1), shape, 0, int(table[amount - 1]))
    standing = jnp.searchsorted(jnp.asarray(table, jnp.int32), pick, side="right")
    return jax.random.permutation(jax.random.fold_in(rng, 2), amount)[standing].astype(jnp.int32)


def bell_draw(stream_key, dims, scale, reach, shards=(), held_as=jnp.bfloat16):
    entries = scale * jax.random.normal(stream_key, dims, jnp.float32)
    if shards:
        entries = entries * shard_levels(stream_key, dims, shards, -0.22, 0.18)
    return jnp.clip(entries, -reach, reach).astype(held_as)


def setup_inputs(seed: int = 0, part: int = 0) -> dict:
    splits = jax.random.split(jax.random.key(seed), 15)
    part_keys = jax.random.split(jax.random.fold_in(splits[14], part), 15)
    enc_input = bell_draw(part_keys[0], (SEQ, D), 1.0, 6.0, ((0, 8),))
    enc_query = draw_enc_query(jax.random.fold_in(jax.random.fold_in(splits[14], part), 71), part)
    enc_key = draw_enc_key(jax.random.fold_in(jax.random.fold_in(splits[14], part), 71), part)
    enc_value = bell_draw(part_keys[3], (SEQ, INNER), 1.0, 6.0, ((0, 8), (1, 2)))
    seq_length = jax.random.randint(part_keys[4], (1,), SEQ // 4, SEQ + 1).astype(jnp.int32)
    attn_out_weight = bell_draw(splits[5], (INNER, D), INNER ** -0.5, 0.1875, ((0, 2),))
    enc_gain = jnp.clip(1.0 + 0.15 * jax.random.normal(splits[6], (D,), jnp.float32), 0.25, 1.75).astype(jnp.bfloat16)
    cross_key_weight = bell_draw(splits[7], (D, INNER), D ** -0.5, 0.09375, ((0, 8), (1, 2)))
    cross_value_weight = bell_draw(splits[8], (D, INNER), D ** -0.5, 0.09375, ((0, 8), (1, 2)))
    embed_table = draw_embed_table(jax.random.fold_in(splits[14], 71), part)
    dec_ids = touch_ends(ranked_ids(part_keys[10], (BEAMS, 2), VOCAB, 2), jax.random.fold_in(part_keys[10], 3), 0, VOCAB - 1).astype(jnp.int32)
    dec_gain = jnp.clip(1.0 + 0.15 * jax.random.normal(splits[11], (D,), jnp.float32), 0.25, 1.75).astype(jnp.bfloat16)
    cross_query_weight = draw_cross_query_weight(jax.random.fold_in(splits[14], 71), part)
    cross_out_weight = bell_draw(splits[13], (INNER, D), INNER ** -0.5, 0.1875, ((0, 2), (1, 8)))
    return dict(enc_input=enc_input, enc_query=enc_query, enc_key=enc_key, enc_value=enc_value, seq_length=seq_length, attn_out_weight=attn_out_weight, enc_gain=enc_gain, cross_key_weight=cross_key_weight, cross_value_weight=cross_value_weight, embed_table=embed_table, dec_ids=dec_ids, dec_gain=dec_gain, cross_query_weight=cross_query_weight, cross_out_weight=cross_out_weight)


EPSILON = 1e-06
FLOOR = -1e+30

def soft_attend(queries, keys, values, valid, factor):
    scores = jnp.einsum('qhd,khd->hqk', queries.astype(jnp.float32), keys) * factor
    scores = jnp.where(valid[None, None, :], scores, FLOOR)
    top = lax.optimization_barrier(jnp.max(scores, axis=-1, keepdims=True))
    probs = jnp.where(valid[None, None, :], jnp.exp(scores - top), 0.0)
    total = lax.optimization_barrier(jnp.sum(probs, axis=-1))
    weights = lax.optimization_barrier(probs.astype(jnp.bfloat16)).astype(jnp.float32)
    mixed = jnp.einsum('hqk,khd->qhd', weights, values)
    return mixed / jnp.transpose(total)[:, :, None]

def reference(enc_input, enc_query, enc_key, enc_value, seq_length, attn_out_weight, enc_gain, cross_key_weight, cross_value_weight, embed_table, dec_ids, dec_gain, cross_query_weight, cross_out_weight):
    valid = jnp.arange(SEQ, dtype=jnp.int32) < seq_length[0]
    block = math.gcd(SEQ, 512)
    keys = enc_key.reshape(SEQ, HEADS, HD).astype(jnp.float32)
    values = enc_value.reshape(SEQ, HEADS, HD).astype(jnp.float32)
    query_blocks = enc_query.reshape(SEQ // block, block, HEADS, HD)

    def one_block(qblk):
        return soft_attend(qblk, keys, values, valid, HD ** (-0.5))
    context = lax.map(one_block, query_blocks).reshape(SEQ, INNER).astype(jnp.bfloat16)
    attended = jnp.dot(context, attn_out_weight, preferred_element_type=jnp.float32)
    resid = enc_input.astype(jnp.float32) + attended
    scale = lax.rsqrt(lax.optimization_barrier(jnp.mean(resid * resid, axis=-1, keepdims=True)) + EPSILON)
    memory = (resid * scale * enc_gain.astype(jnp.float32)).astype(jnp.bfloat16)
    keys_full = jnp.dot(memory, cross_key_weight, preferred_element_type=jnp.float32).astype(jnp.bfloat16)
    values_full = jnp.dot(memory, cross_value_weight, preferred_element_type=jnp.float32).astype(jnp.bfloat16)
    cross_keys = jnp.transpose(keys_full.reshape(SEQ // N_CTX, N_CTX, INNER), (1, 0, 2))
    cross_values = jnp.transpose(values_full.reshape(SEQ // N_CTX, N_CTX, INNER), (1, 0, 2))
    hidden = jnp.take(embed_table, dec_ids.reshape(-1), axis=0).astype(jnp.float32)
    scaled = (hidden * dec_gain.astype(jnp.float32)).astype(jnp.bfloat16)
    raw = jnp.dot(scaled, cross_query_weight, preferred_element_type=jnp.float32)
    factor = lax.rsqrt(lax.optimization_barrier(jnp.sum(hidden * hidden, axis=-1, keepdims=True)) / D + EPSILON)
    query = (raw * factor * HD ** (-0.5)).astype(jnp.bfloat16).reshape(-1, HEADS, HD)
    mixed = soft_attend(query, keys_full.reshape(SEQ, HEADS, HD).astype(jnp.float32), values_full.reshape(SEQ, HEADS, HD).astype(jnp.float32), valid, 1.0)
    attn = mixed.reshape(-1, INNER).astype(jnp.bfloat16)
    out = jnp.dot(attn, cross_out_weight, preferred_element_type=jnp.float32) + hidden
    decoded = out.astype(jnp.bfloat16).reshape(BEAMS, 2, D)
    return (cross_keys, cross_values, decoded)
```

```python
import math

import jax
import jax.numpy as jnp
from jax import lax
from jax.experimental import pallas as pl
from jax.experimental.pallas import tpu as pltpu
from jax.sharding import PartitionSpec as P

D = 4096
HD = 128


EPSILON = 1e-06
FLOOR = -1e30


def joined(value, axis, join):
    pieces = jax.tree.map(lambda part: lax.all_gather(part, axis), value)
    head = jax.tree.map(lambda part: part[0], pieces)
    tail = jax.tree.map(lambda part: part[1:], pieces)
    total, _ = lax.scan(lambda total, piece: (join(total, piece), None), head, tail)
    return total


def softmax_merge(first, second):
    top_first, total_first, mixed_first = first
    top_second, total_second, mixed_second = second
    top = jnp.maximum(top_first, top_second)
    weight_first = jnp.exp(top_first - top)
    weight_second = jnp.exp(top_second - top)
    total = total_first * weight_first + total_second * weight_second
    mixed = mixed_first * weight_first[..., None] + mixed_second * weight_second[..., None]
    return (top, total, mixed)


def partial_softmax(queries, keys, values, valid, factor):
    scores = jnp.einsum("qhd,khd->hqk", queries, keys, preferred_element_type=jnp.float32) * factor
    scores = jnp.where(valid[None, None, :], scores, FLOOR)
    top = jnp.max(scores, axis=-1)
    probs = jnp.where(valid[None, None, :], jnp.exp(scores - top[..., None]), 0.0)
    total = jnp.sum(probs, axis=-1)
    mixed = jnp.einsum(
        "hqk,khd->hqd", probs.astype(jnp.bfloat16), values, preferred_element_type=jnp.float32
    )
    return (top, total, mixed)


def norm_rows(resid, gain):
    scale = lax.rsqrt(jnp.mean(resid * resid, axis=-1, keepdims=True) + EPSILON)
    return (resid * scale * gain.astype(jnp.float32)).astype(jnp.bfloat16)


def local(
    enc_input,
    enc_query,
    enc_key,
    enc_value,
    seq_length,
    attn_out_weight,
    enc_gain,
    cross_key_weight,
    cross_value_weight,
    embed_table,
    dec_ids,
    dec_gain,
    cross_query_weight,
    cross_out_weight,
):
    rows, inner_local = enc_query.shape
    heads_local = inner_local // HD
    limit = seq_length[0]
    queries = enc_query.reshape(rows, heads_local, HD)
    start_state = (
        jnp.full((heads_local, rows), FLOOR, jnp.float32),
        jnp.zeros((heads_local, rows), jnp.float32),
        jnp.zeros((heads_local, rows, HD), jnp.float32),
    )
    carry = start_state
    key_rows = lax.all_gather(enc_key, "ctx", axis=0, tiled=True)
    value_rows = lax.all_gather(enc_value, "ctx", axis=0, tiled=True)
    count = key_rows.shape[0]
    block = math.gcd(count, 2048)
    blocks = count // block
    key_blocks = key_rows.reshape(blocks, block, heads_local, HD)
    value_blocks = value_rows.reshape(blocks, block, heads_local, HD)
    offsets = jnp.arange(blocks, dtype=jnp.int32) * block

    def one_block(state, item):
        key_block, value_block, offset = item
        positions = offset + jnp.arange(block, dtype=jnp.int32)
        update = partial_softmax(queries, key_block, value_block, positions < limit, HD ** (-0.5))
        return (softmax_merge(state, update), None)

    carry, unused = lax.scan(one_block, carry, (key_blocks, value_blocks, offsets))
    top, total, mixed = carry
    context = (
        jnp.transpose(mixed / total[..., None], (1, 0, 2))
        .reshape(rows, inner_local)
        .astype(jnp.bfloat16)
    )
    summed = lax.psum(jnp.dot(context, attn_out_weight, preferred_element_type=jnp.float32), "tp")
    memory = norm_rows(enc_input.astype(jnp.float32) + summed, enc_gain)
    ctx_count = lax.axis_size("ctx")
    slots = rows // ctx_count
    key_sum = jnp.dot(
        memory,
        lax.all_gather(cross_key_weight, "ctx", axis=0, tiled=True),
        preferred_element_type=jnp.float32,
    )
    value_sum = jnp.dot(
        memory,
        lax.all_gather(cross_value_weight, "ctx", axis=0, tiled=True),
        preferred_element_type=jnp.float32,
    )
    key_rows = key_sum.astype(jnp.bfloat16)
    value_rows = value_sum.astype(jnp.bfloat16)
    keys_moved, values_moved = (
        lax.all_to_all(
            key_rows.reshape(slots, ctx_count, inner_local),
            "ctx",
            split_axis=1,
            concat_axis=0,
            tiled=True,
        ),
        lax.all_to_all(
            value_rows.reshape(slots, ctx_count, inner_local),
            "ctx",
            split_axis=1,
            concat_axis=0,
            tiled=True,
        ),
    )
    keys_cache = keys_moved.reshape(rows, inner_local)
    values_cache = values_moved.reshape(rows, inner_local)
    beams = dec_ids.shape[0]
    vocab_local = embed_table.shape[0]
    flat_ids = dec_ids.reshape(-1) - lax.axis_index("tp") * vocab_local
    inside = (flat_ids >= 0) & (flat_ids < vocab_local)
    looked = jnp.take(embed_table, jnp.clip(flat_ids, 0, vocab_local - 1), axis=0)
    own_rows = jnp.where(inside[:, None], looked.astype(jnp.float32), 0.0)
    hidden = lax.psum(own_rows.astype(jnp.bfloat16), "tp").astype(jnp.float32)
    scaled = (hidden * dec_gain.astype(jnp.float32)).astype(jnp.bfloat16)
    raw_part = jnp.dot(scaled, cross_query_weight, preferred_element_type=jnp.float32)
    square_part = jnp.sum(hidden * hidden, axis=-1)
    raw, squares = lax.psum((raw_part, square_part), "ctx")
    factor = lax.rsqrt(squares / D + EPSILON)
    query = (raw * factor[:, None] * HD ** (-0.5)).astype(jnp.bfloat16).reshape(-1, heads_local, HD)
    positions = jnp.arange(rows, dtype=jnp.int32) * ctx_count + lax.axis_index("ctx")
    local_part = partial_softmax(
        query,
        keys_cache.reshape(rows, heads_local, HD),
        values_cache.reshape(rows, heads_local, HD),
        positions < limit,
        1.0,
    )
    top_all, total_all, mixed_all = joined(local_part, "ctx", softmax_merge)
    attn = (
        jnp.transpose(mixed_all / total_all[..., None], (1, 0, 2))
        .reshape(-1, inner_local)
        .astype(jnp.bfloat16)
    )
    out_part = jnp.dot(attn, cross_out_weight, preferred_element_type=jnp.float32)
    out = lax.psum(out_part, "tp")
    decoded = (out + hidden).astype(jnp.bfloat16).reshape(beams, 2, -1)
    return (keys_cache[None], values_cache[None], decoded)


MESH = pl.DeviceIdType.MESH
F32 = jnp.float32
BF16 = jnp.bfloat16
SUBS = 4
CHUNKS = 2


def pick_kernel(ids_ref, table_ref, out_ref, held, rows, sems):
    count = out_ref.shape[0]
    vocab_local = table_ref.shape[0]
    base = lax.axis_index("tp") * vocab_local
    copies = []
    for j in range(count):
        own = jnp.clip(ids_ref[j] - base, 0, vocab_local - 1)
        start = pl.multiple_of(lax.div(own, 16) * 16, 16)
        copy = pltpu.make_async_copy(table_ref.at[pl.ds(start, 16)], held.at[j], sems.at[j])
        copy.start()
        copies.append(copy)
    spots = lax.broadcasted_iota(jnp.int32, held.shape[1:], 0)
    for j in range(count):
        copies[j].wait()
        own = ids_ref[j] - base
        inside = (own >= 0) & (own < vocab_local)
        spot = jnp.where(inside, lax.rem(jnp.clip(own, 0, vocab_local - 1), 16), -1)
        block = held[j].astype(F32)
        rows[pl.ds(j, 1)] = jnp.sum(jnp.where(spots == spot, block, 0.0), axis=0, keepdims=True)
    out_ref[...] = rows[...].astype(BF16)


def fused_kernel(
    q, k, v, ein, looked, dec_gain, wq, wo, enc_gain, wk, wv, wout, valid_enc, valid_dec,
    keys_out, values_out, decoded_out,
    looked_far, wo_all, qg, kg, vg, ein_all, ctx_all, raw_own, raw_out, raw_in, query_in, query_all,
    part_k, part_v, slot_k, slot_v, square_out, square_in,
    mixed_out, mixed_in, stats_out, stats_in, proj_out, proj_in, hidden_ref,
    send, r_look, r_wo, r_q, r_k, r_v, r_raw, r_query, r_ein, r_ein_far, r_ctx, r_square, r_ring, r_mixed,
    r_stats, r_proj,
):
    c = lax.axis_index("ctx")
    t = lax.axis_index("tp")
    z, y = lax.div(c, 2), lax.rem(c, 2)
    mate, other = c + 1 - 2 * y, 1 - t
    line = [lax.rem(z + d, 4) for d in range(1, 4)]
    peers = [lax.rem(c + d, 8) for d in range(1, 8)]
    rows = q.shape[0]
    width = wq.shape[0]
    pending = []

    def put(source, target, arrival, to_ctx, to_tp):
        copy = pltpu.make_async_remote_copy(
            src_ref=source, dst_ref=target, send_sem=send, recv_sem=arrival,
            device_id={"ctx": to_ctx, "tp": to_tp}, device_id_type=MESH,
        )
        copy.start()
        pending.append(copy)

    def got(target, arrival):
        pltpu.make_async_remote_copy(
            src_ref=target, dst_ref=target, send_sem=send, recv_sem=arrival,
            device_id={"ctx": mate, "tp": t}, device_id_type=MESH,
        ).wait_recv()

    def cols(index, size):
        return pl.ds(pl.multiple_of(index * size, size), size)

    barrier = pltpu.get_barrier_semaphore()
    for peer in peers:
        pl.semaphore_signal(barrier, inc=1, device_id={"ctx": peer, "tp": t}, device_id_type=MESH)
    pl.semaphore_signal(barrier, inc=1, device_id={"ctx": c, "tp": other}, device_id_type=MESH)
    pl.semaphore_wait(barrier, len(peers) + 1)

    put(looked, looked_far, r_look, c, other)
    for far in line:
        to = far * 2 + y
        put(k.at[:, cols(far, HD)], kg.at[c], r_k.at[c], to, t)
        put(v.at[:, cols(far, HD)], vg.at[c], r_v.at[c], to, t)
        put(q.at[:, cols(far, HD)], qg.at[z], r_q.at[z], to, t)
    put(k.at[:, cols(z, HD)], kg.at[c], r_k.at[c], mate, t)
    put(v.at[:, cols(z, HD)], vg.at[c], r_v.at[c], mate, t)
    put(wo, wo_all.at[cols(t, wo.shape[0])], r_wo, c, other)
    kg[c] = k[:, cols(z, HD)]
    vg[c] = v[:, cols(z, HD)]
    qg[z] = q[:, cols(z, HD)]
    wo_all[cols(t, wo.shape[0])] = wo[...]
    ein_all[y * 4 + z] = ein[:, cols(c, width)]

    got(looked_far, r_look)
    hidden = looked[...].astype(F32) + looked_far[...].astype(F32)
    hidden_ref[...] = hidden
    scaled = (hidden * dec_gain[...]).astype(BF16)
    inner = wq.shape[1]
    raw_own[:, :inner] = jnp.dot(scaled, wq[...], preferred_element_type=F32)
    raw_own[:, inner:] = jnp.broadcast_to(
        jnp.sum(hidden * hidden, axis=-1, keepdims=True), (hidden.shape[0], 128)
    )
    share = hidden.shape[0] // 8
    for j in range(8):
        raw_out[j] = raw_own[j * share : (j + 1) * share, :]
    for peer in peers:
        put(raw_out.at[peer], raw_in.at[c], r_raw.at[c], peer, t)
    raw_in[c] = raw_out[c]

    for far in line:
        source = far * 2 + y
        got(kg.at[source], r_k.at[source])
        put(kg.at[source], kg.at[source], r_k.at[source], mate, t)
        got(vg.at[source], r_v.at[source])
        put(vg.at[source], vg.at[source], r_v.at[source], mate, t)
    half = rows // 2
    for peer in peers:
        put(
            ein.at[cols(t, half), cols(peer, width)],
            ein_all.at[y * 4 + z, cols(t, half)],
            r_ein.at[c], peer, t,
        )
    for far in line:
        got(qg.at[far], r_q.at[far])
    for far in range(4):
        source = far * 2 + 1 - y
        got(kg.at[source], r_k.at[source])
        got(vg.at[source], r_v.at[source])

    def block(core, head, side, chunk):
        size = 4 * rows // CHUNKS
        place = ctx_all.at[side, pl.ds(chunk * size, size), cols(core * 4 + head, HD)]
        return place, r_ctx.at[(core * 4 + head) * 2 + side, chunk]

    every_key = kg[...].reshape(8 * rows, HD)
    every_value = vg[...].reshape(8 * rows, HD)
    valid = valid_enc[...] > 0.0
    for chunk in range(CHUNKS):
        some = 4 // CHUNKS
        queries = qg[chunk * some : (chunk + 1) * some].reshape(some * rows, HD)
        scores = lax.dot_general(
            queries, every_key, (((1,), (1,)), ((), ())), preferred_element_type=F32
        ) * (HD ** (-0.5))
        scores = jnp.where(valid, scores, FLOOR)
        top = jnp.max(scores, axis=-1, keepdims=True)
        probs = jnp.where(valid, jnp.exp(scores - top), 0.0)
        total = jnp.sum(probs, axis=-1, keepdims=True)
        mixed = jnp.dot(probs.astype(BF16), every_value, preferred_element_type=F32)
        ctx_all[y, pl.ds(chunk * some * rows, some * rows), cols(t * 4 + z, HD)] = (mixed / total).astype(BF16)
        place, arrival = block(t, z, y, chunk)
        for far in line:
            put(place, place, arrival, far * 2 + y, t)
        put(place, place, arrival, mate, t)
        put(place, place, arrival, c, other)

    for peer in peers:
        got(raw_in.at[peer], r_raw.at[peer])
    raw = raw_in[0]
    for j in range(1, 8):
        raw = raw + raw_in[j]
    factor = lax.rsqrt(raw[:, inner : inner + 1] / D + EPSILON)
    query_in[c] = (raw[:, :inner] * factor * HD ** (-0.5)).astype(BF16).astype(F32)
    for peer in peers:
        put(query_in.at[c], query_in.at[c], r_query.at[c], peer, t)

    for peer in peers:
        place = ein_all.at[lax.rem(peer, 2) * 4 + lax.div(peer, 2), cols(t, half)]
        got(place, r_ein.at[peer])
        put(place, place, r_ein_far.at[peer], c, other)
    for chunk in range(CHUNKS):
        for far in line:
            place, arrival = block(t, far, y, chunk)
            got(place, arrival)
            put(place, place, arrival, mate, t)
            put(place, place, arrival, c, other)
    for chunk in range(CHUNKS):
        for far in range(4):
            place, arrival = block(t, far, 1 - y, chunk)
            got(place, arrival)
            put(place, place, arrival, c, other)
    got(wo_all.at[cols(other, wo.shape[0])], r_wo)
    for peer in peers:
        place = ein_all.at[lax.rem(peer, 2) * 4 + lax.div(peer, 2), cols(other, half)]
        got(place, r_ein_far.at[peer])
    for chunk in range(CHUNKS):
        for side in range(2):
            for far in range(4):
                place, arrival = block(other, far, side, chunk)
                got(place, arrival)

    each = rows // 8
    spot_row = lax.broadcasted_iota(jnp.int32, (rows, rows), 0)
    spot_col = lax.broadcasted_iota(jnp.int32, (rows, rows), 1)
    squares = jnp.zeros((8, rows), F32)
    for side in range(2):
        for far in range(4):
            source = far * 2 + side
            resid = jnp.dot(
                ctx_all[side, far * rows : (far + 1) * rows, :], wo_all[...], preferred_element_type=F32
            ) + ein_all[side * 4 + far].astype(F32)
            spread = jnp.where(
                spot_col == source * each + lax.rem(spot_row, each),
                jnp.sum(resid * resid, axis=-1, keepdims=True),
                0.0,
            )
            squares = squares + jnp.sum(spread.reshape(8, each, rows), axis=1)
            gained = (resid * enc_gain[...]).astype(BF16)
            term_k = jnp.dot(gained, wk[...], preferred_element_type=F32).astype(BF16)
            term_v = jnp.dot(gained, wv[...], preferred_element_type=F32).astype(BF16)
            for r in range(8):
                part_k[r, source * each : (source + 1) * each, :] = term_k[r * each : (r + 1) * each]
                part_v[r, source * each : (source + 1) * each, :] = term_v[r * each : (r + 1) * each]
    for r in range(8):
        square_out[r] = squares[r : r + 1]

    def at_ring(place):
        place = lax.rem(place + 16, 8)
        return jnp.where(place < 4, place * 2, (7 - place) * 2 + 1)

    spot = z + y * (7 - 2 * z)
    piece = rows // SUBS
    ways = ((part_k, slot_k, 1), (part_v, slot_v, -1))
    for sub in range(SUBS):
        lines = pl.ds(sub * piece, piece)
        for way, (part, slot, step) in enumerate(ways):
            put(
                part.at[at_ring(spot - step), lines], slot.at[0, lines],
                r_ring.at[way, 0, sub], at_ring(spot + step), t,
            )
    for peer in peers:
        put(square_out.at[peer], square_in.at[c], r_square.at[c], peer, t)
    square_in[c] = square_out[c]
    for peer in peers:
        got(query_in.at[peer], r_query.at[peer])
    for j in range(8):
        query_all[j * share : (j + 1) * share, :] = query_in[j]
    for peer in peers:
        got(square_in.at[peer], r_square.at[peer])
    square = square_in[0]
    for j in range(1, 8):
        square = square + square_in[j]
    column = jnp.sum(jnp.where(spot_row == spot_col, square, 0.0), axis=-1, keepdims=True)
    scale = lax.rsqrt(column / D + EPSILON)

    for hop in range(7):
        for sub in range(SUBS):
            lines = pl.ds(sub * piece, piece)
            for way, (part, slot, step) in enumerate(ways):
                got(slot.at[hop, lines], r_ring.at[way, hop, sub])
                here = part[at_ring(spot - step * (hop + 2)), lines].astype(F32)
                running = slot[hop, lines].astype(F32) + here
                if hop < 6:
                    slot[hop, lines] = running.astype(BF16)
                    put(
                        slot.at[hop, lines], slot.at[hop + 1, lines],
                        r_ring.at[way, hop + 1, sub], at_ring(spot + step), t,
                    )
                else:
                    out = keys_out if way == 0 else values_out
                    out[lines] = (running * scale[sub * piece : (sub + 1) * piece]).astype(BF16)

    own_valid = valid_dec[...] > 0.0
    lanes = lax.broadcasted_iota(jnp.int32, stats_out.shape, 1)
    stats = jnp.zeros(stats_out.shape, F32)
    heads = inner // HD
    for head in range(heads):
        part = slice(head * HD, (head + 1) * HD)
        scores = lax.dot_general(
            query_all[:, part].astype(BF16), keys_out[:, part], (((1,), (1,)), ((), ())),
            preferred_element_type=F32,
        )
        scores = jnp.where(own_valid, scores, FLOOR)
        top = jnp.max(scores, axis=-1, keepdims=True)
        probs = jnp.where(own_valid, jnp.exp(scores - top), 0.0)
        stats = jnp.where(lanes == head, top, stats)
        stats = jnp.where(lanes == heads + head, jnp.sum(probs, axis=-1, keepdims=True), stats)
        mixed_out[:, part] = jnp.dot(
            probs.astype(BF16), values_out[:, part], preferred_element_type=F32
        ).astype(BF16)
    stats_out[...] = stats
    for peer in peers:
        put(stats_out, stats_in.at[c], r_stats.at[c], peer, t)
        put(mixed_out, mixed_in.at[c], r_mixed.at[c], peer, t)
    stats_in[c] = stats_out[...]
    mixed_in[c] = mixed_out[...]
    for peer in peers:
        got(stats_in.at[peer], r_stats.at[peer])
        got(mixed_in.at[peer], r_mixed.at[peer])
    proj = jnp.zeros(proj_out.shape, F32)
    for head in range(heads):
        part = slice(head * HD, (head + 1) * HD)
        tops = [stats_in[j][:, head : head + 1] for j in range(8)]
        top = tops[0]
        for j in range(1, 8):
            top = jnp.maximum(top, tops[j])
        total = jnp.zeros_like(top)
        mixed = jnp.zeros((top.shape[0], HD), F32)
        for j in range(8):
            weight = jnp.exp(tops[j] - top)
            total = total + stats_in[j][:, heads + head : heads + head + 1] * weight
            mixed = mixed + mixed_in[j][:, part].astype(F32) * weight
        proj = proj + jnp.dot((mixed / total).astype(BF16), wout[part, :], preferred_element_type=F32)
    proj_out[...] = proj
    put(proj_out, proj_in, r_proj, c, other)
    got(proj_in, r_proj)
    decoded_out[...] = (proj_out[...] + proj_in[...] + hidden_ref[...]).astype(BF16)
    for copy in pending:
        copy.wait_send()


def local_fused(
    enc_input, enc_query, enc_key, enc_value, seq_length, attn_out_weight, enc_gain, cross_key_weight,
    cross_value_weight, embed_table, dec_ids, dec_gain, cross_query_weight, cross_out_weight,
):
    rows, inner = enc_query.shape
    width = cross_query_weight.shape[0]
    c = lax.axis_index("ctx")
    tokens = dec_ids.size
    whole = pl.BlockSpec(memory_space=pltpu.VMEM)
    looked = pl.pallas_call(
        pick_kernel,
        out_shape=jax.ShapeDtypeStruct((tokens, width), BF16),
        in_specs=[pl.BlockSpec(memory_space=pltpu.SMEM), pl.BlockSpec(memory_space=pl.ANY)],
        out_specs=whole,
        scratch_shapes=[
            pltpu.VMEM((tokens, 16, width), BF16),
            pltpu.VMEM((tokens, width), F32),
            pltpu.SemaphoreType.DMA((tokens,)),
        ],
    )(dec_ids.reshape(-1), embed_table)
    order = jnp.arange(rows, dtype=jnp.int32)
    wanted = (order % (rows // 8)) * 8 + order // (rows // 8)
    turn = (wanted[:, None] == order[None, :]).astype(BF16)
    query = jnp.dot(turn, enc_query, preferred_element_type=F32).astype(BF16)
    ein = jnp.dot(turn, enc_input, preferred_element_type=F32).astype(BF16)
    wo = lax.dynamic_slice_in_dim(attn_out_weight, c * width, width, 1)
    gain = lax.dynamic_slice_in_dim(enc_gain, c * width, width, 0).astype(F32)[None]
    limit = seq_length[0]
    valid_enc = (jnp.arange(8 * rows, dtype=jnp.int32) < limit).astype(F32)[None]
    valid_dec = (order * 8 + c < limit).astype(F32)[None]
    dma = pltpu.SemaphoreType.DMA
    share = tokens // 8
    keys, values, decoded = pl.pallas_call(
        fused_kernel,
        out_shape=(
            jax.ShapeDtypeStruct((rows, inner), BF16),
            jax.ShapeDtypeStruct((rows, inner), BF16),
            jax.ShapeDtypeStruct((tokens, width), BF16),
        ),
        in_specs=[whole] * 14,
        out_specs=(whole, whole, whole),
        scratch_shapes=[
            pltpu.VMEM((tokens, width), BF16),
            pltpu.VMEM((2 * inner, width), BF16),
            pltpu.VMEM((4, rows, HD), BF16),
            pltpu.VMEM((8, rows, HD), BF16),
            pltpu.VMEM((8, rows, HD), BF16),
            pltpu.VMEM((8, rows, width), BF16),
            pltpu.VMEM((2, 4 * rows, 2 * inner), BF16),
            pltpu.VMEM((tokens, inner + 128), F32),
            pltpu.VMEM((8, share, inner + 128), F32),
            pltpu.VMEM((8, share, inner + 128), F32),
            pltpu.VMEM((8, share, inner), F32),
            pltpu.VMEM((tokens, inner), F32),
            pltpu.VMEM((8, rows, inner), BF16),
            pltpu.VMEM((8, rows, inner), BF16),
            pltpu.VMEM((7, rows, inner), BF16),
            pltpu.VMEM((7, rows, inner), BF16),
            pltpu.VMEM((8, 1, rows), F32),
            pltpu.VMEM((8, 1, rows), F32),
            pltpu.VMEM((tokens, inner), BF16),
            pltpu.VMEM((8, tokens, inner), BF16),
            pltpu.VMEM((tokens, 128), F32),
            pltpu.VMEM((8, tokens, 128), F32),
            pltpu.VMEM((tokens, width), F32),
            pltpu.VMEM((tokens, width), F32),
            pltpu.VMEM((tokens, width), F32),
            dma, dma, dma, dma((4,)), dma((8,)), dma((8,)), dma((8,)), dma((8,)), dma((8,)), dma((8,)),
            dma((16, CHUNKS)), dma((8,)), dma((2, 7, SUBS)), dma((8,)), dma((8,)), dma,
        ],
        compiler_params=pltpu.CompilerParams(
            collective_id=0, has_side_effects=True, vmem_limit_bytes=60 * 1024 * 1024
        ),
    )(
        query, enc_key, enc_value, ein, looked, dec_gain.astype(F32)[None], cross_query_weight, wo, gain,
        cross_key_weight, cross_value_weight, cross_out_weight, valid_enc, valid_dec,
    )
    return keys[None], values[None], decoded.reshape(dec_ids.shape[0], 2, width)


def chosen(*arrays):
    rows, inner = arrays[1].shape
    fits = lax.axis_size("ctx") == 8 and lax.axis_size("tp") == 2 and (rows, inner) == (128, 4 * HD)
    return (local_fused if fits else local)(*arrays)


def solution(mesh):
    placed = (
        P(("groups", "ctx"), None),
        P(("groups", "ctx"), "tp"),
        P(("groups", "ctx"), "tp"),
        P(("groups", "ctx"), "tp"),
        P("groups"),
        P("tp", None),
        P(),
        P("ctx", "tp"),
        P("ctx", "tp"),
        P("tp", "ctx"),
        P("groups", None),
        P("ctx"),
        P("ctx", "tp"),
        P("tp", "ctx"),
    )
    return jax.shard_map(
        chosen,
        mesh=mesh,
        in_specs=placed,
        out_specs=(
            P(("groups", "ctx"), None, "tp"),
            P(("groups", "ctx"), None, "tp"),
            P("groups", None, "ctx"),
        ),
        check_vma=False,
    )
```

```python
import math

import jax
import jax.numpy as jnp
from jax import lax
from jax.experimental import pallas as pl
from jax.experimental.pallas import tpu as pltpu
from jax.sharding import PartitionSpec as P

D = 4096
HD = 128


EPSILON = 1e-06
FLOOR = -1e30


def joined(value, axis, join):
    pieces = jax.tree.map(lambda part: lax.all_gather(part, axis), value)
    head = jax.tree.map(lambda part: part[0], pieces)
    tail = jax.tree.map(lambda part: part[1:], pieces)
    total, _ = lax.scan(lambda total, piece: (join(total, piece), None), head, tail)
    return total


def softmax_merge(first, second):
    top_first, total_first, mixed_first = first
    top_second, total_second, mixed_second = second
    top = jnp.maximum(top_first, top_second)
    weight_first = jnp.exp(top_first - top)
    weight_second = jnp.exp(top_second - top)
    total = total_first * weight_first + total_second * weight_second
    mixed = mixed_first * weight_first[..., None] + mixed_second * weight_second[..., None]
    return (top, total, mixed)


def partial_softmax(queries, keys, values, valid, factor):
    scores = jnp.einsum("qhd,khd->hqk", queries, keys, preferred_element_type=jnp.float32) * factor
    scores = jnp.where(valid[None, None, :], scores, FLOOR)
    top = jnp.max(scores, axis=-1)
    probs = jnp.where(valid[None, None, :], jnp.exp(scores - top[..., None]), 0.0)
    total = jnp.sum(probs, axis=-1)
    mixed = jnp.einsum(
        "hqk,khd->hqd", probs.astype(jnp.bfloat16), values, preferred_element_type=jnp.float32
    )
    return (top, total, mixed)


def norm_rows(resid, gain):
    scale = lax.rsqrt(jnp.mean(resid * resid, axis=-1, keepdims=True) + EPSILON)
    return (resid * scale * gain.astype(jnp.float32)).astype(jnp.bfloat16)


def local(
    enc_input,
    enc_query,
    enc_key,
    enc_value,
    seq_length,
    attn_out_weight,
    enc_gain,
    cross_key_weight,
    cross_value_weight,
    embed_table,
    dec_ids,
    dec_gain,
    cross_query_weight,
    cross_out_weight,
):
    rows, inner_local = enc_query.shape
    heads_local = inner_local // HD
    limit = seq_length[0]
    queries = enc_query.reshape(rows, heads_local, HD)
    start_state = (
        jnp.full((heads_local, rows), FLOOR, jnp.float32),
        jnp.zeros((heads_local, rows), jnp.float32),
        jnp.zeros((heads_local, rows, HD), jnp.float32),
    )
    carry = start_state
    key_rows = lax.all_gather(enc_key, "ctx", axis=0, tiled=True)
    value_rows = lax.all_gather(enc_value, "ctx", axis=0, tiled=True)
    count = key_rows.shape[0]
    block = math.gcd(count, 2048)
    blocks = count // block
    key_blocks = key_rows.reshape(blocks, block, heads_local, HD)
    value_blocks = value_rows.reshape(blocks, block, heads_local, HD)
    offsets = jnp.arange(blocks, dtype=jnp.int32) * block

    def one_block(state, item):
        key_block, value_block, offset = item
        positions = offset + jnp.arange(block, dtype=jnp.int32)
        update = partial_softmax(queries, key_block, value_block, positions < limit, HD ** (-0.5))
        return (softmax_merge(state, update), None)

    carry, unused = lax.scan(one_block, carry, (key_blocks, value_blocks, offsets))
    top, total, mixed = carry
    context = (
        jnp.transpose(mixed / total[..., None], (1, 0, 2))
        .reshape(rows, inner_local)
        .astype(jnp.bfloat16)
    )
    summed = lax.psum(jnp.dot(context, attn_out_weight, preferred_element_type=jnp.float32), "tp")
    memory = norm_rows(enc_input.astype(jnp.float32) + summed, enc_gain)
    ctx_count = lax.axis_size("ctx")
    slots = rows // ctx_count
    key_sum = jnp.dot(
        memory,
        lax.all_gather(cross_key_weight, "ctx", axis=0, tiled=True),
        preferred_element_type=jnp.float32,
    )
    value_sum = jnp.dot(
        memory,
        lax.all_gather(cross_value_weight, "ctx", axis=0, tiled=True),
        preferred_element_type=jnp.float32,
    )
    key_rows = key_sum.astype(jnp.bfloat16)
    value_rows = value_sum.astype(jnp.bfloat16)
    keys_moved, values_moved = (
        lax.all_to_all(
            key_rows.reshape(slots, ctx_count, inner_local),
            "ctx",
            split_axis=1,
            concat_axis=0,
            tiled=True,
        ),
        lax.all_to_all(
            value_rows.reshape(slots, ctx_count, inner_local),
            "ctx",
            split_axis=1,
            concat_axis=0,
            tiled=True,
        ),
    )
    keys_cache = keys_moved.reshape(rows, inner_local)
    values_cache = values_moved.reshape(rows, inner_local)
    beams = dec_ids.shape[0]
    vocab_local = embed_table.shape[0]
    flat_ids = dec_ids.reshape(-1) - lax.axis_index("tp") * vocab_local
    inside = (flat_ids >= 0) & (flat_ids < vocab_local)
    looked = jnp.take(embed_table, jnp.clip(flat_ids, 0, vocab_local - 1), axis=0)
    own_rows = jnp.where(inside[:, None], looked.astype(jnp.float32), 0.0)
    hidden = lax.psum(own_rows.astype(jnp.bfloat16), "tp").astype(jnp.float32)
    scaled = (hidden * dec_gain.astype(jnp.float32)).astype(jnp.bfloat16)
    raw_part = jnp.dot(scaled, cross_query_weight, preferred_element_type=jnp.float32)
    square_part = jnp.sum(hidden * hidden, axis=-1)
    raw, squares = lax.psum((raw_part, square_part), "ctx")
    factor = lax.rsqrt(squares / D + EPSILON)
    query = (raw * factor[:, None] * HD ** (-0.5)).astype(jnp.bfloat16).reshape(-1, heads_local, HD)
    positions = jnp.arange(rows, dtype=jnp.int32) * ctx_count + lax.axis_index("ctx")
    local_part = partial_softmax(
        query,
        keys_cache.reshape(rows, heads_local, HD),
        values_cache.reshape(rows, heads_local, HD),
        positions < limit,
        1.0,
    )
    top_all, total_all, mixed_all = joined(local_part, "ctx", softmax_merge)
    attn = (
        jnp.transpose(mixed_all / total_all[..., None], (1, 0, 2))
        .reshape(-1, inner_local)
        .astype(jnp.bfloat16)
    )
    out_part = jnp.dot(attn, cross_out_weight, preferred_element_type=jnp.float32)
    out = lax.psum(out_part, "tp")
    decoded = (out + hidden).astype(jnp.bfloat16).reshape(beams, 2, -1)
    return (keys_cache[None], values_cache[None], decoded)


MESH = pl.DeviceIdType.MESH
F32 = jnp.float32
BF16 = jnp.bfloat16
SUBS = 4
CHUNKS = 2


def pick_kernel(ids_ref, length_ref, table_ref, out_ref, enc_mask, dec_mask, held, rows, sems):
    count = out_ref.shape[0]
    vocab_local = table_ref.shape[0]
    base = lax.axis_index("tp") * vocab_local
    copies = []
    for j in range(count):
        own = jnp.clip(ids_ref[j] - base, 0, vocab_local - 1)
        start = pl.multiple_of(lax.div(own, 16) * 16, 16)
        copy = pltpu.make_async_copy(table_ref.at[pl.ds(start, 16)], held.at[j], sems.at[j])
        copy.start()
        copies.append(copy)
    limit = length_ref[0]
    enc_mask[...] = (lax.broadcasted_iota(jnp.int32, enc_mask.shape, 1) < limit).astype(F32)
    places = lax.broadcasted_iota(jnp.int32, dec_mask.shape, 1) * 8 + lax.axis_index("ctx")
    dec_mask[...] = (places < limit).astype(F32)
    spots = lax.broadcasted_iota(jnp.int32, held.shape[1:], 0)
    for j in range(count):
        copies[j].wait()
        own = ids_ref[j] - base
        inside = (own >= 0) & (own < vocab_local)
        spot = jnp.where(inside, lax.rem(jnp.clip(own, 0, vocab_local - 1), 16), -1)
        block = held[j].astype(F32)
        rows[pl.ds(j, 1)] = jnp.sum(jnp.where(spots == spot, block, 0.0), axis=0, keepdims=True)
    out_ref[...] = rows[...].astype(BF16)


def hand_kernel(keys_ref, values_ref, decoded_ref, keys_out, values_out, decoded_out):
    keys_out[0] = keys_ref[...]
    values_out[0] = values_ref[...]
    for i in range(decoded_out.shape[0]):
        decoded_out[i] = decoded_ref[2 * i : 2 * i + 2].astype(BF16)


def fused_kernel(
    q, k, v, ein, looked, dec_gain, wq, wo, enc_gain, wk_far, wv_far, wout_far, valid_enc, valid_dec,
    keys_out, values_out, decoded_out,
    looked_far, wo_all, qg, kg, vg, ein_all, ctx_all, raw_own, raw_out, raw_in, query_in, query_all,
    wk, wv, wout, gained_all, part_k, part_v, slot_k, slot_v, square_out, square_in,
    mixed_out, mixed_in, stats_out, stats_in, proj_out, proj_in, hidden_ref,
    send, r_look, r_wo, r_q, r_k, r_v, r_raw, r_query, r_ein, r_ein_far, r_ctx, r_square, r_ring, r_mixed,
    r_stats, r_proj, fetched,
):
    c = lax.axis_index("ctx")
    t = lax.axis_index("tp")
    z, y = lax.div(c, 2), lax.rem(c, 2)
    mate, other = c + 1 - 2 * y, 1 - t
    line = [lax.rem(z + d, 4) for d in range(1, 4)]
    peers = [lax.rem(c + d, 8) for d in range(1, 8)]
    rows = q.shape[0]
    width = wq.shape[0]
    pending = []

    def put(source, target, arrival, to_ctx, to_tp):
        copy = pltpu.make_async_remote_copy(
            src_ref=source, dst_ref=target, send_sem=send, recv_sem=arrival,
            device_id={"ctx": to_ctx, "tp": to_tp}, device_id_type=MESH,
        )
        copy.start()
        pending.append(copy)

    def got(target, arrival):
        pltpu.make_async_remote_copy(
            src_ref=target, dst_ref=target, send_sem=send, recv_sem=arrival,
            device_id={"ctx": mate, "tp": t}, device_id_type=MESH,
        ).wait_recv()

    def fetch(source, target, arrival):
        copy = pltpu.make_async_copy(source, target, arrival)
        copy.start()
        return copy

    def cols(index, size):
        return pl.ds(pl.multiple_of(index * size, size), size)

    barrier = pltpu.get_barrier_semaphore()
    for peer in peers:
        pl.semaphore_signal(barrier, inc=1, device_id={"ctx": peer, "tp": t}, device_id_type=MESH)
    pl.semaphore_signal(barrier, inc=1, device_id={"ctx": c, "tp": other}, device_id_type=MESH)
    pl.semaphore_wait(barrier, len(peers) + 1)

    put(looked, looked_far, r_look, c, other)
    for far in line:
        to = far * 2 + y
        put(k.at[:, cols(far, HD)], kg.at[c], r_k.at[c], to, t)
        put(v.at[:, cols(far, HD)], vg.at[c], r_v.at[c], to, t)
        put(q.at[:, cols(far, HD)], qg.at[z], r_q.at[z], to, t)
    put(k.at[:, cols(z, HD)], kg.at[c], r_k.at[c], mate, t)
    put(v.at[:, cols(z, HD)], vg.at[c], r_v.at[c], mate, t)
    put(wo.at[:, cols(c, width)], wo_all.at[cols(t, wo.shape[0])], r_wo, c, other)
    fetches = [
        fetch(wo.at[:, cols(c, width)], wo_all.at[cols(t, wo.shape[0])], fetched.at[0]),
        fetch(ein.at[:, cols(c, width)], ein_all.at[y * 4 + z], fetched.at[1]),
        fetch(wk_far, wk, fetched.at[2]),
        fetch(wv_far, wv, fetched.at[3]),
        fetch(wout_far, wout, fetched.at[4]),
    ]
    kg[c] = k[:, cols(z, HD)]
    vg[c] = v[:, cols(z, HD)]
    qg[z] = q[:, cols(z, HD)]

    got(looked_far, r_look)
    hidden = looked[...].astype(F32) + looked_far[...].astype(F32)
    hidden_ref[...] = hidden
    scaled = (hidden * dec_gain[...].astype(F32)).astype(BF16)
    inner = wq.shape[1]
    raw_own[:, :inner] = jnp.dot(scaled, wq[...], preferred_element_type=F32)
    raw_own[:, inner:] = jnp.broadcast_to(
        jnp.sum(hidden * hidden, axis=-1, keepdims=True), (hidden.shape[0], 128)
    )
    share = hidden.shape[0] // 8
    for j in range(8):
        raw_out[j] = raw_own[j * share : (j + 1) * share, :]
    for peer in peers:
        put(raw_out.at[peer], raw_in.at[c], r_raw.at[c], peer, t)
    raw_in[c] = raw_out[c]

    for far in line:
        source = far * 2 + y
        got(kg.at[source], r_k.at[source])
        put(kg.at[source], kg.at[source], r_k.at[source], mate, t)
        got(vg.at[source], r_v.at[source])
        put(vg.at[source], vg.at[source], r_v.at[source], mate, t)
    half = rows // 2
    for peer in peers:
        put(
            ein.at[cols(t, half), cols(peer, width)],
            ein_all.at[y * 4 + z, cols(t, half)],
            r_ein.at[c], peer, t,
        )
    for far in line:
        got(qg.at[far], r_q.at[far])
    for far in range(4):
        source = far * 2 + 1 - y
        got(kg.at[source], r_k.at[source])
        got(vg.at[source], r_v.at[source])

    def block(core, head, side, chunk):
        size = 4 * rows // CHUNKS
        place = ctx_all.at[side, pl.ds(chunk * size, size), cols(core * 4 + head, HD)]
        return place, r_ctx.at[(core * 4 + head) * 2 + side, chunk]

    every_key = kg[...].reshape(8 * rows, HD)
    every_value = vg[...].reshape(8 * rows, HD)
    valid = valid_enc[...] > 0.0
    for chunk in range(CHUNKS):
        some = 4 // CHUNKS
        queries = qg[chunk * some : (chunk + 1) * some].reshape(some * rows, HD)
        scores = lax.dot_general(
            queries, every_key, (((1,), (1,)), ((), ())), preferred_element_type=F32
        ) * (HD ** (-0.5))
        scores = jnp.where(valid, scores, FLOOR)
        top = jnp.max(scores, axis=-1, keepdims=True)
        probs = jnp.where(valid, jnp.exp(scores - top), 0.0)
        total = jnp.sum(probs, axis=-1, keepdims=True)
        mixed = jnp.dot(probs.astype(BF16), every_value, preferred_element_type=F32)
        ctx_all[y, pl.ds(chunk * some * rows, some * rows), cols(t * 4 + z, HD)] = (mixed / total).astype(BF16)
        place, arrival = block(t, z, y, chunk)
        for far in line:
            put(place, place, arrival, far * 2 + y, t)
        put(place, place, arrival, mate, t)
        put(place, place, arrival, c, other)

    for peer in peers:
        got(raw_in.at[peer], r_raw.at[peer])
    raw = raw_in[0]
    for j in range(1, 8):
        raw = raw + raw_in[j]
    factor = lax.rsqrt(raw[:, inner : inner + 1] / D + EPSILON)
    query_in[c] = (raw[:, :inner] * factor * HD ** (-0.5)).astype(BF16).astype(F32)
    for peer in peers:
        put(query_in.at[c], query_in.at[c], r_query.at[c], peer, t)

    for peer in peers:
        place = ein_all.at[lax.rem(peer, 2) * 4 + lax.div(peer, 2), cols(t, half)]
        got(place, r_ein.at[peer])
        put(place, place, r_ein_far.at[peer], c, other)
    for chunk in range(CHUNKS):
        for far in line:
            place, arrival = block(t, far, y, chunk)
            got(place, arrival)
            put(place, place, arrival, mate, t)
            put(place, place, arrival, c, other)
    for chunk in range(CHUNKS):
        for far in range(4):
            place, arrival = block(t, far, 1 - y, chunk)
            got(place, arrival)
            put(place, place, arrival, c, other)
    got(wo_all.at[cols(other, wo.shape[0])], r_wo)
    for peer in peers:
        place = ein_all.at[lax.rem(peer, 2) * 4 + lax.div(peer, 2), cols(other, half)]
        got(place, r_ein_far.at[peer])
    for copy in fetches:
        copy.wait()

    each = rows // 8
    spot_row = lax.broadcasted_iota(jnp.int32, (rows, rows), 0)
    spot_col = lax.broadcasted_iota(jnp.int32, (rows, rows), 1)
    turn = (spot_col == lax.rem(spot_row, each) * 8 + lax.div(spot_row, each)).astype(BF16)
    picked = lax.broadcasted_iota(jnp.int32, enc_gain.shape, 0) == c
    gain = jnp.sum(jnp.where(picked, enc_gain[...].astype(F32), 0.0), axis=0, keepdims=True)
    squares = jnp.zeros((8, rows), F32)
    for chunk in range(CHUNKS):
        for side in range(2):
            for far in range(4):
                place, arrival = block(other, far, side, chunk)
                got(place, arrival)
        for side in range(2):
            for far in range(chunk * 4 // CHUNKS, (chunk + 1) * 4 // CHUNKS):
                source = far * 2 + side
                resid = jnp.dot(
                    ctx_all[side, far * rows : (far + 1) * rows, :], wo_all[...], preferred_element_type=F32
                ) + ein_all[side * 4 + far].astype(F32)
                spread = jnp.where(
                    spot_col == source * each + lax.div(spot_row, 8),
                    jnp.sum(resid * resid, axis=-1, keepdims=True),
                    0.0,
                )
                squares = squares + jnp.sum(spread.reshape(each, 8, rows), axis=0)
                gained = (resid * gain).astype(BF16)
                moved = jnp.dot(turn, gained, preferred_element_type=F32).astype(BF16)
                for r in range(8):
                    gained_all[r, source * each : (source + 1) * each, :] = moved[r * each : (r + 1) * each]
    for r in range(8):
        square_out[r] = squares[r : r + 1]

    def at_ring(place):
        place = lax.rem(place + 16, 8)
        return jnp.where(place < 4, place * 2, (7 - place) * 2 + 1)

    spot = z + y * (7 - 2 * z)
    piece = rows // SUBS
    ways = ((part_k, slot_k, 1, wk), (part_v, slot_v, -1, wv))

    def term(hop):
        for part, slot, step, weight in ways:
            own = gained_all[at_ring(spot - step * (hop + 1))]
            part[hop] = jnp.dot(own, weight[...], preferred_element_type=F32).astype(BF16)

    term(0)
    for sub in range(SUBS):
        lines = pl.ds(sub * piece, piece)
        for way, (part, slot, step, weight) in enumerate(ways):
            put(
                part.at[0, lines], slot.at[0, lines],
                r_ring.at[way, 0, sub], at_ring(spot + step), t,
            )
    for peer in peers:
        put(square_out.at[peer], square_in.at[c], r_square.at[c], peer, t)
    square_in[c] = square_out[c]
    for peer in peers:
        got(query_in.at[peer], r_query.at[peer])
    for j in range(8):
        query_all[j * share : (j + 1) * share, :] = query_in[j]
    for peer in peers:
        got(square_in.at[peer], r_square.at[peer])
    square = square_in[0]
    for j in range(1, 8):
        square = square + square_in[j]
    column = jnp.sum(jnp.where(spot_row == spot_col, square, 0.0), axis=-1, keepdims=True)
    scale = lax.rsqrt(column / D + EPSILON)

    term(1)
    for hop in range(7):
        for sub in range(SUBS):
            lines = pl.ds(sub * piece, piece)
            for way, (part, slot, step, weight) in enumerate(ways):
                got(slot.at[hop, lines], r_ring.at[way, hop, sub])
                here = part[hop + 1, lines].astype(F32)
                running = slot[hop, lines].astype(F32) + here
                if hop < 6:
                    slot[hop, lines] = running.astype(BF16)
                    put(
                        slot.at[hop, lines], slot.at[hop + 1, lines],
                        r_ring.at[way, hop + 1, sub], at_ring(spot + step), t,
                    )
                else:
                    out = keys_out if way == 0 else values_out
                    out[lines] = (running * scale[sub * piece : (sub + 1) * piece]).astype(BF16)
        if hop < 6:
            term(hop + 2)

    own_valid = valid_dec[...] > 0.0
    lanes = lax.broadcasted_iota(jnp.int32, stats_out.shape, 1)
    stats = jnp.zeros(stats_out.shape, F32)
    heads = inner // HD
    for head in range(heads):
        part = slice(head * HD, (head + 1) * HD)
        scores = lax.dot_general(
            query_all[:, part].astype(BF16), keys_out[:, part], (((1,), (1,)), ((), ())),
            preferred_element_type=F32,
        )
        scores = jnp.where(own_valid, scores, FLOOR)
        top = jnp.max(scores, axis=-1, keepdims=True)
        probs = jnp.where(own_valid, jnp.exp(scores - top), 0.0)
        stats = jnp.where(lanes == head, top, stats)
        stats = jnp.where(lanes == heads + head, jnp.sum(probs, axis=-1, keepdims=True), stats)
        mixed_out[:, part] = jnp.dot(
            probs.astype(BF16), values_out[:, part], preferred_element_type=F32
        ).astype(BF16)
    stats_out[...] = stats
    for peer in peers:
        put(stats_out, stats_in.at[c], r_stats.at[c], peer, t)
        put(mixed_out, mixed_in.at[c], r_mixed.at[c], peer, t)
    stats_in[c] = stats_out[...]
    mixed_in[c] = mixed_out[...]
    for peer in peers:
        got(stats_in.at[peer], r_stats.at[peer])
        got(mixed_in.at[peer], r_mixed.at[peer])
    proj = jnp.zeros(proj_out.shape, F32)
    for head in range(heads):
        part = slice(head * HD, (head + 1) * HD)
        tops = [stats_in[j][:, head : head + 1] for j in range(8)]
        top = tops[0]
        for j in range(1, 8):
            top = jnp.maximum(top, tops[j])
        total = jnp.zeros_like(top)
        mixed = jnp.zeros((top.shape[0], HD), F32)
        for j in range(8):
            weight = jnp.exp(tops[j] - top)
            total = total + stats_in[j][:, heads + head : heads + head + 1] * weight
            mixed = mixed + mixed_in[j][:, part].astype(F32) * weight
        proj = proj + jnp.dot((mixed / total).astype(BF16), wout[part, :], preferred_element_type=F32)
    proj_out[...] = proj
    put(proj_out, proj_in, r_proj, c, other)
    got(proj_in, r_proj)
    decoded_out[...] = proj_out[...] + proj_in[...] + hidden_ref[...]
    for copy in pending:
        copy.wait_send()


def local_fused(
    enc_input, enc_query, enc_key, enc_value, seq_length, attn_out_weight, enc_gain, cross_key_weight,
    cross_value_weight, embed_table, dec_ids, dec_gain, cross_query_weight, cross_out_weight,
):
    rows, inner = enc_query.shape
    width = cross_query_weight.shape[0]
    tokens = dec_ids.size
    whole = pl.BlockSpec(memory_space=pltpu.VMEM)
    scalars = pl.BlockSpec(memory_space=pltpu.SMEM)
    anywhere = pl.BlockSpec(memory_space=pl.ANY)
    looked, valid_enc, valid_dec = pl.pallas_call(
        pick_kernel,
        out_shape=(
            jax.ShapeDtypeStruct((tokens, width), BF16),
            jax.ShapeDtypeStruct((1, 8 * rows), F32),
            jax.ShapeDtypeStruct((1, rows), F32),
        ),
        in_specs=[scalars, scalars, anywhere],
        out_specs=(whole, whole, whole),
        scratch_shapes=[
            pltpu.VMEM((tokens, 16, width), BF16),
            pltpu.VMEM((tokens, width), F32),
            pltpu.SemaphoreType.DMA((tokens,)),
        ],
    )(dec_ids.reshape(-1), seq_length, embed_table)
    dma = pltpu.SemaphoreType.DMA
    share = tokens // 8
    keys, values, decoded = pl.pallas_call(
        fused_kernel,
        out_shape=(
            jax.ShapeDtypeStruct((rows, inner), BF16),
            jax.ShapeDtypeStruct((rows, inner), BF16),
            jax.ShapeDtypeStruct((tokens, width), F32),
        ),
        in_specs=[
            whole, whole, whole, anywhere, whole, whole, whole, anywhere, whole, anywhere, anywhere, anywhere,
            whole, whole,
        ],
        out_specs=(whole, whole, whole),
        scratch_shapes=[
            pltpu.VMEM((tokens, width), BF16),
            pltpu.VMEM((2 * inner, width), BF16),
            pltpu.VMEM((4, rows, HD), BF16),
            pltpu.VMEM((8, rows, HD), BF16),
            pltpu.VMEM((8, rows, HD), BF16),
            pltpu.VMEM((8, rows, width), BF16),
            pltpu.VMEM((2, 4 * rows, 2 * inner), BF16),
            pltpu.VMEM((tokens, inner + 128), F32),
            pltpu.VMEM((8, share, inner + 128), F32),
            pltpu.VMEM((8, share, inner + 128), F32),
            pltpu.VMEM((8, share, inner), F32),
            pltpu.VMEM((tokens, inner), F32),
            pltpu.VMEM((width, inner), BF16),
            pltpu.VMEM((width, inner), BF16),
            pltpu.VMEM((inner, width), BF16),
            pltpu.VMEM((8, rows, width), BF16),
            pltpu.VMEM((8, rows, inner), BF16),
            pltpu.VMEM((8, rows, inner), BF16),
            pltpu.VMEM((7, rows, inner), BF16),
            pltpu.VMEM((7, rows, inner), BF16),
            pltpu.VMEM((8, 1, rows), F32),
            pltpu.VMEM((8, 1, rows), F32),
            pltpu.VMEM((tokens, inner), BF16),
            pltpu.VMEM((8, tokens, inner), BF16),
            pltpu.VMEM((tokens, 128), F32),
            pltpu.VMEM((8, tokens, 128), F32),
            pltpu.VMEM((tokens, width), F32),
            pltpu.VMEM((tokens, width), F32),
            pltpu.VMEM((tokens, width), F32),
            dma, dma, dma, dma((4,)), dma((8,)), dma((8,)), dma((8,)), dma((8,)), dma((8,)), dma((8,)),
            dma((16, CHUNKS)), dma((8,)), dma((2, 7, SUBS)), dma((8,)), dma((8,)), dma, dma((5,)),
        ],
        compiler_params=pltpu.CompilerParams(
            collective_id=0, has_side_effects=True, vmem_limit_bytes=60 * 1024 * 1024
        ),
    )(
        enc_query, enc_key, enc_value, enc_input, looked, dec_gain[None], cross_query_weight, attn_out_weight,
        enc_gain.reshape(8, width),
        cross_key_weight, cross_value_weight, cross_out_weight, valid_enc, valid_dec,
    )
    return pl.pallas_call(
        hand_kernel,
        out_shape=(
            jax.ShapeDtypeStruct((1, rows, inner), BF16),
            jax.ShapeDtypeStruct((1, rows, inner), BF16),
            jax.ShapeDtypeStruct((tokens // 2, 2, width), BF16),
        ),
        in_specs=[whole] * 3,
        out_specs=(whole, whole, whole),
    )(keys, values, decoded)


def chosen(*arrays):
    rows, inner = arrays[1].shape
    fits = lax.axis_size("ctx") == 8 and lax.axis_size("tp") == 2 and (rows, inner) == (128, 4 * HD)
    return (local_fused if fits else local)(*arrays)


def solution(mesh):
    placed = (
        P(("groups", "ctx"), None),
        P(("groups", "ctx"), "tp"),
        P(("groups", "ctx"), "tp"),
        P(("groups", "ctx"), "tp"),
        P("groups"),
        P("tp", None),
        P(),
        P("ctx", "tp"),
        P("ctx", "tp"),
        P("tp", "ctx"),
        P("groups", None),
        P("ctx"),
        P("ctx", "tp"),
        P("tp", "ctx"),
    )
    return jax.shard_map(
        chosen,
        mesh=mesh,
        in_specs=placed,
        out_specs=(
            P(("groups", "ctx"), None, "tp"),
            P(("groups", "ctx"), None, "tp"),
            P("groups", None, "ctx"),
        ),
        check_vma=False,
    )
```
